32 devices in a mesh: side: 2 (over core), dev: 16 (over z, y, x).
Axes of the slice: x: 2, y: 2, z: 4, core: 2. Of those that a mesh axis runs over, the one named last changes fastest.
Arguments:
- queries: bfloat16 [512, 4096], P(('side', 'dev')), may hold values from -150 to 150
- cached_key_table: bfloat16 [512, 256, 256], P(('side', 'dev')), may hold values from -6 to 6
- cached_value_table: bfloat16 [512, 256, 256], P(('side', 'dev')), may hold values from -12 to 12
- incoming_keys: bfloat16 [512, 256], P(('side', 'dev')), may hold values from -6 to 6
- incoming_values: bfloat16 [512, 256], P(('side', 'dev')), may hold values from -12 to 12
- context_length_per_row: int32 [512], P(('side', 'dev')), may hold values from 1 to 256, as said below
- residual: bfloat16 [512, 4096], P(('side', 'dev')), may hold values from -2 to 2
- norm_gain: bfloat16 [4096], replicated, may hold values from 0.099609375 to 1.8984375
- expert_ids: int32 [512, 8], P(('side', 'dev')), may hold values from 0 to 15, all different within a row; in each aligned block of 16 rows (0 to 15, 16 to 31, ...) at most 16 rows name the same one
- gate_weights: float32 [512, 8], P(('side', 'dev')), may hold values from 0.05 to 0.5
- gate_proj: bfloat16 [16, 4096, 1536], P('dev', None, 'side'), may hold values from -0.09375 to 0.09375
- up_proj: bfloat16 [16, 4096, 1536], P('dev', None, 'side'), may hold values from -0.09375 to 0.09375
- down_proj: bfloat16 [16, 1536, 4096], P('dev', 'side'), may hold values from -0.15625 to 0.15625
Outputs:
- layer_out: bfloat16 [512, 4096], P(('side', 'dev'))
The draws below stay inside these ranges and needn't reach their ends.
Inputs may be any that keep to these rules, and one draw needn't show every extreme that they name: `context_length_per_row`: some row uses all 256 cached positions. `expert_ids`: each row names 8 different experts; among the rows of one device no expert is named more than 16 times, a bound that some block reaches.
All inputs are finite; a program needn't handle non-finite values.
Results may differ from the reference program's by a relative error of at most 0.011.
Values may be sent and summed in bfloat16 or wider, within the bound.
A program may use at most 128 MiB of HBM per device.

```python
import math
import jax
import jax.numpy as jnp
import numpy as np
from jax import lax

D = 4096
QUERY_HEADS = 32
KEY_VALUE_HEADS = 2
HEAD_SIZE = 128
FF = 1536
TOPK = 8
DEVICE_ROWS = 16
CONTEXT_SLOTS = 256
EXPERTS = 16
TOKEN_TOTAL = 512
CAP = 16
N_DEV = 16


def shared_keys(key):
    return jnp.clip(jax.random.normal(jax.random.fold_in(key, 11), (TOKEN_TOTAL, CONTEXT_SLOTS, KEY_VALUE_HEADS * HEAD_SIZE), jnp.float32), -6.0, 6.0)


def draw_cached_key_table(key, part):
    return shared_keys(key).astype(jnp.bfloat16)


def draw_queries(key, part):
    base = jnp.clip(jax.random.normal(jax.random.fold_in(key, 12), (TOKEN_TOTAL, QUERY_HEADS, HEAD_SIZE), jnp.float32), -6.0, 6.0)
    return base.reshape(TOKEN_TOTAL, QUERY_HEADS * HEAD_SIZE).astype(jnp.bfloat16)


def draw_context_length_per_row(key, part):
    drawn = jax.random.randint(jax.random.fold_in(key, 21), (TOKEN_TOTAL,), 1, CONTEXT_SLOTS + 1, dtype=jnp.int32)
    return drawn.at[0].set(CONTEXT_SLOTS)


def level_of(rng, shape, split, low, largest):
    def one(axis_at, shards_of):
        steps = jax.random.uniform(jax.random.fold_in(jax.random.fold_in(rng, 6), axis_at), (shards_of,), jnp.float32, low / len(split), largest / len(split))
        return jnp.repeat(jnp.exp(steps), shape[axis_at] // shards_of).reshape((-1,) + (1,) * (len(shape) - axis_at - 1))

    level = one(*split[0])
    for cut in split[1:]:
        level = level * one(*cut)
    return level


def routed_block(key, own, number, rows, count, top, reach, lean):
    ranking = jax.random.permutation(key, count)
    packed, common = portions_of(count, rows * top, reach, lean, True), portions_of(count, rows * top, reach, lean, False)
    places = jnp.arange(count)

    def named(sizes, offset_by):
        used = int((sizes > 0).sum())
        fixed = max(1, used // 4)
        passed = fixed + (places - fixed + offset_by * (used - fixed)) % max(1, count - fixed)
        return jnp.zeros((count,), jnp.int32).at[ranking[jnp.where(places < fixed, places, passed)]].set(jnp.asarray(sizes, jnp.int32))

    sizes = jnp.where(number % 4 == 0, named(packed, number // 4), named(common, number - number // 4 - 1))
    mixed = jax.random.permutation(jax.random.fold_in(own, 3), count)
    donor, receiver = mixed[0:count // 2 * 2:2], mixed[1:count // 2 * 2:2]
    margin = jnp.minimum(sizes[donor] - 1, reach - sizes[receiver]) // 2
    margin = jnp.where((donor == ranking[0]) | (receiver == ranking[0]) | (sizes[receiver] == 0), 0, jnp.maximum(margin, 0))
    passed = jax.random.randint(jax.random.fold_in(own, 4), (count // 2,), 0, 1 << 20) % (margin + 1)
    sizes = sizes.at[donor].add(-passed).at[receiver].add(passed)
    items = jnp.searchsorted(jnp.cumsum(sizes), jnp.arange(rows * top), side="right").astype(jnp.int32)
    grid = items.reshape(top, rows).T
    grid = grid[jax.random.permutation(jax.random.fold_in(own, 1), rows)]
    offset_by = jax.random.randint(jax.random.fold_in(own, 2), (rows, 1), 0, top)
    return jnp.take_along_axis(grid, (jnp.arange(top)[None, :] + offset_by) % top, axis=1)


def portions_of(amount, total, most, skew, full):
    loads = [(1 << 20) // math.isqrt(rank ** skew) + 1 for rank in range(1, amount + 1)]
    largest = most if full else min(most, max(-(-total // amount), total * loads[0] // sum(loads)))
    least = 1 if total - largest >= amount - 1 else 0
    given, surplus = [largest] + [least] * (amount - 1), total - largest - least * (amount - 1)
    while surplus > 0:
        movable = [i for i in range(1, amount) if given[i] < largest] or [i for i in range(1, amount) if given[i] < most]
        mass, budget = sum([loads[i] for i in movable]), surplus
        for i in movable:
            more = min(most - given[i], max(1, budget * loads[i] // mass), surplus)
            given[i] = given[i] + more
            surplus = surplus - more
    return np.array(given)


def normal_values(rng, extent, deviation, most, cuts=(), kind=jnp.bfloat16):
    gain = level_of(rng, extent, cuts, -0.22, 0.18) if cuts else 1.0
    entries = jax.random.normal(rng, extent, jnp.float32) * deviation * gain
    return jnp.minimum(jnp.maximum(entries, -most), most).astype(kind)


def setup_inputs(seed: int = 0) -> dict:
    streams_of = jax.random.split(jax.random.key(seed), 14)
    queries = draw_queries(jax.random.fold_in(streams_of[13], 71), 0)
    cached_key_table = draw_cached_key_table(jax.random.fold_in(streams_of[13], 71), 0)
    cached_value_table = normal_values(streams_of[2], (TOKEN_TOTAL, CONTEXT_SLOTS, KEY_VALUE_HEADS * HEAD_SIZE), 2.0, 12.0, ((0, 32),))
    incoming_keys = normal_values(streams_of[3], (TOKEN_TOTAL, KEY_VALUE_HEADS * HEAD_SIZE), 1.0, 6.0, ((0, 32),))
    incoming_values = normal_values(streams_of[4], (TOKEN_TOTAL, KEY_VALUE_HEADS * HEAD_SIZE), 2.0, 12.0, ((0, 32),))
    context_length_per_row = draw_context_length_per_row(jax.random.fold_in(streams_of[13], 71), 0)
    residual = normal_values(streams_of[6], (TOKEN_TOTAL, D), 0.3, 2.0, ((0, 32),))
    norm_gain = jnp.clip(1.0 + 0.18 * jax.random.normal(streams_of[7], (D,), jnp.float32), 0.099609375, 1.8984375).astype(jnp.bfloat16)
    expert_ids_keys = jax.random.split(jax.random.fold_in(streams_of[8], 1), TOKEN_TOTAL // DEVICE_ROWS)
    expert_ids_turns = jax.random.permutation(jax.random.fold_in(streams_of[8], 3), TOKEN_TOTAL // DEVICE_ROWS)
    expert_ids = jax.vmap(lambda own, number: routed_block(jax.random.fold_in(streams_of[8], 2), own, number, DEVICE_ROWS, EXPERTS, TOPK, CAP, 2))(expert_ids_keys, expert_ids_turns).reshape((TOKEN_TOTAL, TOPK))
    gate_weights = jnp.clip(jnp.exp(math.log(0.5) - 2.3025851 * jax.random.uniform(streams_of[9], (TOKEN_TOTAL, TOPK), jnp.float32) ** level_of(streams_of[9], (TOKEN_TOTAL, TOPK), ((0, 32),), -0.2, 0.2)), 0.05, 0.5)
    gate_proj = normal_values(streams_of[10], (EXPERTS, D, FF), D ** -0.5, 0.09375, ((0, 16), (2, 2)))
    up_proj = normal_values(streams_of[11], (EXPERTS, D, FF), D ** -0.5, 0.09375, ((0, 16), (2, 2)))
    down_proj = normal_values(streams_of[12], (EXPERTS, FF, D), FF ** -0.5, 0.15625, ((0, 16), (1, 2)))
    return {"queries": queries, "cached_key_table": cached_key_table, "cached_value_table": cached_value_table, "incoming_keys": incoming_keys, "incoming_values": incoming_values, "context_length_per_row": context_length_per_row, "residual": residual, "norm_gain": norm_gain, "expert_ids": expert_ids, "gate_weights": gate_weights, "gate_proj": gate_proj, "up_proj": up_proj, "down_proj": down_proj}


def attend(queries, cached_key_table, cached_value_table, incoming_keys, incoming_values, context_length_per_row):
    count_of_rows, span_length, _ = cached_key_table.shape
    heads_of_queries = queries.astype(jnp.float32).reshape(count_of_rows, KEY_VALUE_HEADS, QUERY_HEADS // KEY_VALUE_HEADS, HEAD_SIZE)
    heads_of_keys = cached_key_table.astype(jnp.float32).reshape(count_of_rows, span_length, KEY_VALUE_HEADS, HEAD_SIZE)
    heads_of_values = cached_value_table.astype(jnp.float32).reshape(count_of_rows, span_length, KEY_VALUE_HEADS, HEAD_SIZE)
    newest_key = incoming_keys.astype(jnp.float32).reshape(count_of_rows, KEY_VALUE_HEADS, HEAD_SIZE)
    newest_value = incoming_values.astype(jnp.float32).reshape(count_of_rows, KEY_VALUE_HEADS, HEAD_SIZE)
    score_scale = HEAD_SIZE ** (-0.5)
    cached = jnp.einsum('rkgd,rlkd->rkgl', heads_of_queries, heads_of_keys) * score_scale
    fresh = jnp.einsum('rkgd,rkd->rkg', heads_of_queries, newest_key) * score_scale
    valid_mask = jnp.arange(span_length, dtype=jnp.int32)[None, :] < context_length_per_row[:, None]
    cached = jnp.where(valid_mask[:, None, None, :], cached, jnp.float32(-1e+30))
    top_score = jnp.maximum(lax.optimization_barrier(jnp.max(cached, axis=-1)), fresh)
    exp_cached = jnp.exp(cached - top_score[..., None])
    exp_fresh = jnp.exp(fresh - top_score)
    denominator = lax.optimization_barrier(jnp.sum(exp_cached, axis=-1)) + exp_fresh
    prob_cached = (exp_cached / denominator[..., None]).astype(jnp.bfloat16)
    prob_fresh = (exp_fresh / denominator).astype(jnp.bfloat16)
    mixed = jnp.einsum('rkgl,rlkd->rkgd', prob_cached.astype(jnp.float32), heads_of_values)
    mixed = mixed + prob_fresh.astype(jnp.float32)[..., None] * newest_value[:, :, None, :]
    return mixed.reshape(count_of_rows, QUERY_HEADS * HEAD_SIZE)

def reference(queries, cached_key_table, cached_value_table, incoming_keys, incoming_values, context_length_per_row, residual, norm_gain, expert_ids, gate_weights, gate_proj, up_proj, down_proj):
    count_of_blocks = TOKEN_TOTAL // DEVICE_ROWS
    packed_rows_result = (queries.reshape(count_of_blocks, DEVICE_ROWS, QUERY_HEADS * HEAD_SIZE), cached_key_table.reshape(count_of_blocks, DEVICE_ROWS, CONTEXT_SLOTS, KEY_VALUE_HEADS * HEAD_SIZE), cached_value_table.reshape(count_of_blocks, DEVICE_ROWS, CONTEXT_SLOTS, KEY_VALUE_HEADS * HEAD_SIZE), incoming_keys.reshape(count_of_blocks, DEVICE_ROWS, KEY_VALUE_HEADS * HEAD_SIZE), incoming_values.reshape(count_of_blocks, DEVICE_ROWS, KEY_VALUE_HEADS * HEAD_SIZE), context_length_per_row.reshape(count_of_blocks, DEVICE_ROWS))
    attn = lax.map(lambda pack: attend(*pack), packed_rows_result).reshape(TOKEN_TOTAL, QUERY_HEADS * HEAD_SIZE)
    hidden = (residual.astype(jnp.float32) + attn).astype(jnp.bfloat16)
    wide = hidden.astype(jnp.float32)
    mean_square = lax.optimization_barrier(jnp.mean(wide * wide, axis=-1, keepdims=True))
    normed = (wide * lax.rsqrt(mean_square + 1e-06) * norm_gain.astype(jnp.float32)).astype(jnp.bfloat16)
    pair_count = TOKEN_TOTAL * TOPK
    flat_ids = expert_ids.reshape(pair_count)
    flat_weights = gate_weights.reshape(pair_count).astype(jnp.float32)
    row_of = jnp.arange(pair_count, dtype=jnp.int32) // TOPK
    bound = 2 * N_DEV * CAP

    def one_expert(accum, pack):
        expert, gate_mat, up_mat, down_mat = pack
        match = flat_ids == expert
        rank = jnp.cumsum(match.astype(jnp.int32)) - 1
        target = jnp.where(match, rank, bound).astype(jnp.int32)
        index = jnp.zeros((bound,), jnp.int32).at[target].set(jnp.arange(pair_count, dtype=jnp.int32), mode='drop')
        weight = jnp.zeros((bound,), flat_weights.dtype).at[target].set(flat_weights, mode='drop')
        rows_in = normed[row_of[index]]
        gate_val = jnp.dot(rows_in, gate_mat, preferred_element_type=jnp.float32)
        up_val = jnp.dot(rows_in, up_mat, preferred_element_type=jnp.float32)
        act = (jax.nn.silu(gate_val) * up_val).astype(jnp.bfloat16)
        output = jnp.dot(act, down_mat, preferred_element_type=jnp.float32).astype(jnp.bfloat16)
        accum = accum.at[row_of[index]].add(weight[:, None] * output.astype(jnp.float32))
        return (accum, None)
    start = jnp.zeros((TOKEN_TOTAL, D), jnp.float32)
    moe_sum, _ = lax.scan(one_expert, start, (jnp.arange(EXPERTS, dtype=jnp.int32), gate_proj, up_proj, down_proj))
    return (hidden.astype(jnp.float32) + moe_sum).astype(jnp.bfloat16)
```

```python
import jax
import jax.numpy as jnp
from jax import lax
from jax.sharding import PartitionSpec as P

QUERY_HEADS = 32
KEY_VALUE_HEADS = 2
HEAD_SIZE = 128


def attend(
    queries,
    cached_key_table,
    cached_value_table,
    incoming_keys,
    incoming_values,
    context_length_per_row,
):
    count_of_rows, span_length, _ = cached_key_table.shape
    heads_of_queries = queries.reshape(
        count_of_rows, KEY_VALUE_HEADS, QUERY_HEADS // KEY_VALUE_HEADS, HEAD_SIZE
    )
    heads_of_keys = cached_key_table.reshape(count_of_rows, span_length, KEY_VALUE_HEADS, HEAD_SIZE)
    heads_of_values = cached_value_table.reshape(
        count_of_rows, span_length, KEY_VALUE_HEADS, HEAD_SIZE
    )
    newest_key = incoming_keys.reshape(count_of_rows, KEY_VALUE_HEADS, HEAD_SIZE)
    newest_value = incoming_values.reshape(count_of_rows, KEY_VALUE_HEADS, HEAD_SIZE)
    score_scale = HEAD_SIZE ** (-0.5)
    cached = (
        jnp.einsum(
            "rkgd,rlkd->rkgl", heads_of_queries, heads_of_keys, preferred_element_type=jnp.float32
        )
        * score_scale
    )
    fresh = (
        jnp.einsum(
            "rkgd,rkd->rkg", heads_of_queries, newest_key, preferred_element_type=jnp.float32
        )
        * score_scale
    )
    valid_mask = jnp.arange(span_length, dtype=jnp.int32)[None, :] < context_length_per_row[:, None]
    cached = jnp.where(valid_mask[:, None, None, :], cached, jnp.float32(-1e30))
    top_score = jnp.maximum(jnp.max(cached, axis=-1), fresh)
    exp_cached = jnp.exp(cached - top_score[..., None])
    exp_fresh = jnp.exp(fresh - top_score)
    denominator = jnp.sum(exp_cached, axis=-1) + exp_fresh
    prob_cached = (exp_cached / denominator[..., None]).astype(jnp.bfloat16)
    prob_fresh = (exp_fresh / denominator).astype(jnp.bfloat16)
    mixed = jnp.einsum(
        "rkgl,rlkd->rkgd", prob_cached, heads_of_values, preferred_element_type=jnp.float32
    )
    mixed = (
        mixed
        + prob_fresh.astype(jnp.float32)[..., None]
        * newest_value.astype(jnp.float32)[:, :, None, :]
    )
    return mixed.reshape(count_of_rows, QUERY_HEADS * HEAD_SIZE)


def weight_columns(chosen_ids, gate_weights, expert_count):
    experts = jnp.arange(expert_count, dtype=jnp.int32)
    table = jnp.sum(
        jnp.where(chosen_ids[:, :, None] == experts, gate_weights[:, :, None], 0.0), axis=1
    )
    high = table.astype(jnp.bfloat16)
    low = (table - high.astype(jnp.float32)).astype(jnp.bfloat16)
    columns = jnp.concatenate([high, low], axis=1)
    return jnp.pad(columns, ((0, 0), (0, -columns.shape[1] % 128)))


def on_device(
    queries,
    cached_key_table,
    cached_value_table,
    incoming_keys,
    incoming_values,
    context_length_per_row,
    residual,
    norm_gain,
    expert_ids,
    gate_weights,
    gate_proj,
    up_proj,
    down_proj,
):
    count_of_rows, width = residual.shape
    expert_count = lax.axis_size("dev")
    attn = attend(
        queries,
        cached_key_table,
        cached_value_table,
        incoming_keys,
        incoming_values,
        context_length_per_row,
    )
    hidden = (residual.astype(jnp.float32) + attn).astype(jnp.bfloat16)
    wide = hidden.astype(jnp.float32)
    mean_square = jnp.mean(wide * wide, axis=-1, keepdims=True)
    normed = (wide * lax.rsqrt(mean_square + 1e-06) * norm_gain.astype(jnp.float32)).astype(
        jnp.bfloat16
    )
    mine = lax.axis_index("dev")
    sent = jnp.concatenate([normed, weight_columns(expert_ids, gate_weights, expert_count)], axis=1)
    rows = lax.all_gather(sent, ("side", "dev"), axis=0, tiled=True)
    tail = rows[:, width:].astype(jnp.float32)
    places = jnp.arange(tail.shape[1], dtype=jnp.int32)
    weight = jnp.sum(
        jnp.where((places == mine) | (places == mine + expert_count), tail, 0.0),
        axis=1,
        keepdims=True,
    )
    rows = rows[:, :width]
    gate_val = jnp.dot(rows, gate_proj[0], preferred_element_type=jnp.float32)
    up_val = jnp.dot(rows, up_proj[0], preferred_element_type=jnp.float32)
    act = (jax.nn.silu(gate_val) * up_val).astype(jnp.bfloat16)
    part = jnp.dot(act, down_proj[0], preferred_element_type=jnp.float32)
    part = (part * weight).astype(jnp.bfloat16)
    summed = lax.psum_scatter(part, ("side", "dev"), scatter_dimension=0, tiled=True)
    return (hidden.astype(jnp.float32) + summed.astype(jnp.float32)).astype(jnp.bfloat16)


def solution(mesh):
    in_specs = (
        P(("side", "dev"), None),
        P(("side", "dev"), None, None),
        P(("side", "dev"), None, None),
        P(("side", "dev"), None),
        P(("side", "dev"), None),
        P(("side", "dev")),
        P(("side", "dev"), None),
        P(),
        P(("side", "dev"), None),
        P(("side", "dev"), None),
        P("dev", None, "side"),
        P("dev", None, "side"),
        P("dev", "side", None),
    )
    out_specs = P(("side", "dev"), None)
    return jax.shard_map(
        on_device, mesh=mesh, in_specs=in_specs, out_specs=out_specs, check_vma=False
    )
```

```python
import functools

import jax
import jax.numpy as jnp
from jax import lax
from jax.experimental import pallas as pl
from jax.experimental.pallas import tpu as pltpu
from jax.sharding import PartitionSpec as P

QUERY_HEADS = 32
KEY_VALUE_HEADS = 2
HEAD_SIZE = 128
MESH = pl.DeviceIdType.MESH
VMEM_LIMIT = 60 * 1024 * 1024


def grid_of(count):
    return {16: (4, 2, 2), 64: (4, 4, 4)}.get(count, (count, 1, 1))


def halves_of(width):
    first = width // 256 * 128
    return (slice(0, first), slice(first, width))


class Links:
    def __init__(self, sizes):
        self.sizes = sizes
        me = lax.axis_index("dev")
        self.side = lax.axis_index("side")
        self.at = (me // (sizes[1] * sizes[2]), me // sizes[2] % sizes[1], me % sizes[2])
        self.started = []

    def moved(self, steps):
        spot = [(a + n + d) % n for a, d, n in zip(self.at, steps, self.sizes)]
        return (spot[0] * self.sizes[1] + spot[1]) * self.sizes[2] + spot[2]

    def along(self, axis, step):
        return {"dev": self.moved(tuple(step if i == axis else 0 for i in range(3)))}

    def other(self):
        return {"side": 1 - self.side}

    def barrier(self):
        semaphore = pltpu.get_barrier_semaphore()
        peers = [self.other()]
        for axis in range(3):
            peers += [self.along(axis, step) for step in range(1, self.sizes[axis])]
        for peer in peers:
            pl.semaphore_signal(semaphore, inc=1, device_id=peer, device_id_type=MESH)
        pl.semaphore_wait(semaphore, len(peers))

    def copy(self, source, target, send_sems, recv_sem, peer):
        sent = pltpu.make_async_remote_copy(
            src_ref=source,
            dst_ref=target,
            send_sem=send_sems.at[len(self.started)],
            recv_sem=recv_sem,
            device_id=peer,
            device_id_type=MESH,
        )
        sent.start()
        self.started.append(sent)

    def arrived(self, target, send_sems, recv_sem):
        pltpu.make_async_remote_copy(
            src_ref=target,
            dst_ref=target,
            send_sem=send_sems.at[0],
            recv_sem=recv_sem,
            device_id=self.other(),
            device_id_type=MESH,
        ).wait_recv()

    def finish(self):
        for sent in self.started:
            sent.wait_send()


def gather_kernel(sizes, own_ref, all_ref, send_sems, near_sems, mid_sems, far_sems, side_sems):
    n0, n1, n2 = sizes
    count = n0 * n1 * n2
    links = Links(sizes)
    cuts = halves_of(own_ref.shape[1])
    links.barrier()

    def block(steps, half, side=None):
        base = (links.side if side is None else side) * count
        return all_ref.at[base + links.moved(steps), :, cuts[half]]

    def source(steps, half):
        return own_ref.at[:, cuts[half]] if steps == (0, 0, 0) else block(steps, half)

    def relative(steps):
        back = [-d % n for d, n in zip(steps, sizes)]
        return (back[0] * n1 + back[1]) * n2 + back[2]

    def cross(steps, half):
        links.copy(
            source(steps, half), block(steps, half), send_sems,
            side_sems.at[half, relative(steps)], links.other(),
        )

    def spread(steps, half, axis, sems, slot):
        for k in range(1, sizes[axis]):
            links.copy(
                source(steps, half), block(steps, half), send_sems,
                sems.at[half, slot * max(sizes) + k], links.along(axis, k),
            )

    first, second = (2, 1), (1, 2)
    for half in range(2):
        for k in range(1, n0):
            links.copy(
                source((0, 0, 0), half), block((0, 0, 0), half), send_sems,
                near_sems.at[half, k], links.along(0, k),
            )
    for j in range(n0):
        for half in range(2):
            steps = (-j, 0, 0)
            if j:
                links.arrived(block(steps, half), send_sems, near_sems.at[half, j])
            spread(steps, half, first[half], mid_sems, j)
            spread(steps, half, second[half], far_sems, j * max(sizes))
            cross(steps, half)

    def shifted(j, half, mid, far):
        steps = [-j, 0, 0]
        steps[first[half]] = -mid
        steps[second[half]] = -far
        return tuple(steps)

    for j in range(n0):
        for half in range(2):
            for k in range(1, sizes[first[half]]):
                steps = shifted(j, half, k, 0)
                links.arrived(block(steps, half), send_sems, mid_sems.at[half, j * max(sizes) + k])
                spread(steps, half, second[half], far_sems, j * max(sizes) + k)
                cross(steps, half)
    for j in range(n0):
        for c in range(max(sizes)):
            for half in range(2):
                if c >= sizes[first[half]]:
                    continue
                for k in range(1, sizes[second[half]]):
                    steps = shifted(j, half, c, k)
                    slot = (j * max(sizes) + c) * max(sizes) + k
                    links.arrived(block(steps, half), send_sems, far_sems.at[half, slot])
                    cross(steps, half)
    all_ref[links.side * count + links.moved((0, 0, 0))] = own_ref[...]
    for j in range(n0):
        for b in range(n1):
            for c in range(n2):
                for half in range(2):
                    steps = (-j, -b, -c)
                    links.arrived(
                        block(steps, half, 1 - links.side), send_sems,
                        side_sems.at[half, relative(steps)],
                    )
    links.finish()


def gather_rows(own):
    count = lax.axis_size("dev")
    sizes = grid_of(count)
    wide = max(sizes)
    rows, width = own.shape
    dma = pltpu.SemaphoreType.DMA
    sends = 2 * (count - 1) + 2 * count
    return pl.pallas_call(
        functools.partial(gather_kernel, sizes),
        out_shape=jax.ShapeDtypeStruct((2 * count, rows, width), own.dtype),
        in_specs=[pl.BlockSpec(memory_space=pltpu.VMEM)],
        out_specs=pl.BlockSpec(memory_space=pltpu.VMEM),
        scratch_shapes=[
            dma((sends,)),
            dma((2, wide)),
            dma((2, wide * wide)),
            dma((2, wide * wide * wide)),
            dma((2, count)),
        ],
        compiler_params=pltpu.CompilerParams(
            collective_id=0, has_side_effects=True, vmem_limit_bytes=VMEM_LIMIT
        ),
        name="gather_rows",
    )(own).reshape(2 * count * rows, width)


def sum_kernel(
    sizes, part_ref, out_ref, acc, from_side, from_far, from_mid, from_near,
    send_sems, side_sems, far_sems, mid_sems, near_sems,
):
    n0, n1, n2 = sizes
    count = n0 * n1 * n2
    wide = max(sizes)
    links = Links(sizes)
    cuts = halves_of(out_ref.shape[1])
    first, second = (2, 1), (1, 2)
    links.barrier()
    order = [(j, b, c) for b in range(n1 - 1, -1, -1) for c in range(n2 - 1, -1, -1) for j in range(n0)]

    def mine(steps):
        return links.moved(steps)

    for i, steps in enumerate(order):
        links.copy(
            part_ref.at[(1 - links.side) * count + mine(steps)], from_side.at[i],
            send_sems, side_sems.at[i], links.other(),
        )

    def total(left, right):
        return (left.astype(jnp.float32) + right.astype(jnp.float32)).astype(jnp.bfloat16)

    for i, steps in enumerate(order):
        spot = mine(steps)
        links.arrived(from_side.at[i], send_sems, side_sems.at[i])
        acc[spot] = total(part_ref[links.side * count + spot], from_side[i])
        for half in range(2):
            k = steps[second[half]]
            if k:
                slot = (steps[0] * wide + steps[first[half]]) * wide + k
                links.copy(
                    acc.at[spot, :, cuts[half]], from_far.at[half, slot],
                    send_sems, far_sems.at[half, slot], links.along(second[half], k),
                )

    def shifted(j, half, mid):
        steps = [j, 0, 0]
        steps[first[half]] = mid
        return tuple(steps)

    for c in range(wide - 1, -1, -1):
        for j in range(n0):
            for half in range(2):
                if c >= sizes[first[half]]:
                    continue
                spot = mine(shifted(j, half, c))
                for k in range(1, sizes[second[half]]):
                    slot = (j * wide + c) * wide + k
                    links.arrived(from_far.at[half, slot], send_sems, far_sems.at[half, slot])
                    acc[spot, :, cuts[half]] = total(
                        acc[spot, :, cuts[half]], from_far[half, slot]
                    )
                if c:
                    slot = j * wide + c
                    links.copy(
                        acc.at[spot, :, cuts[half]], from_mid.at[half, slot],
                        send_sems, mid_sems.at[half, slot], links.along(first[half], c),
                    )
    for j in range(n0 - 1, -1, -1):
        for half in range(2):
            spot = mine((j, 0, 0))
            for k in range(1, sizes[first[half]]):
                slot = j * wide + k
                links.arrived(from_mid.at[half, slot], send_sems, mid_sems.at[half, slot])
                acc[spot, :, cuts[half]] = total(acc[spot, :, cuts[half]], from_mid[half, slot])
            if j:
                links.copy(
                    acc.at[spot, :, cuts[half]], from_near.at[half, j],
                    send_sems, near_sems.at[half, j], links.along(0, j),
                )
    for half in range(2):
        value = acc[mine((0, 0, 0)), :, cuts[half]].astype(jnp.float32)
        for k in range(1, n0):
            links.arrived(from_near.at[half, k], send_sems, near_sems.at[half, k])
            value = value + from_near[half, k].astype(jnp.float32)
        out_ref[:, cuts[half]] = value
    links.finish()


def sum_rows(part):
    count = lax.axis_size("dev")
    sizes = grid_of(count)
    wide = max(sizes)
    _, rows, width = part.shape
    dma = pltpu.SemaphoreType.DMA
    slots = sizes[0] * wide
    return pl.pallas_call(
        functools.partial(sum_kernel, sizes),
        out_shape=jax.ShapeDtypeStruct((rows, width), jnp.float32),
        in_specs=[pl.BlockSpec(memory_space=pltpu.VMEM)],
        out_specs=pl.BlockSpec(memory_space=pltpu.VMEM),
        scratch_shapes=[
            pltpu.VMEM((count, rows, width), part.dtype),
            pltpu.VMEM((count, rows, width), part.dtype),
            pltpu.VMEM((2, slots * wide, rows, width // 2), part.dtype),
            pltpu.VMEM((2, slots, rows, width // 2), part.dtype),
            pltpu.VMEM((2, sizes[0], rows, width // 2), part.dtype),
            dma((count + 2 * (count - 1),)),
            dma((count,)),
            dma((2, slots * wide)),
            dma((2, slots)),
            dma((2, sizes[0])),
        ],
        compiler_params=pltpu.CompilerParams(
            collective_id=1, has_side_effects=True, vmem_limit_bytes=VMEM_LIMIT
        ),
        name="sum_rows",
    )(part)


def attend(
    queries,
    cached_key_table,
    cached_value_table,
    incoming_keys,
    incoming_values,
    context_length_per_row,
):
    count_of_rows, span_length, _ = cached_key_table.shape
    heads_of_queries = queries.reshape(
        count_of_rows, KEY_VALUE_HEADS, QUERY_HEADS // KEY_VALUE_HEADS, HEAD_SIZE
    )
    heads_of_keys = cached_key_table.reshape(count_of_rows, span_length, KEY_VALUE_HEADS, HEAD_SIZE)
    heads_of_values = cached_value_table.reshape(
        count_of_rows, span_length, KEY_VALUE_HEADS, HEAD_SIZE
    )
    newest_key = incoming_keys.reshape(count_of_rows, KEY_VALUE_HEADS, HEAD_SIZE)
    newest_value = incoming_values.reshape(count_of_rows, KEY_VALUE_HEADS, HEAD_SIZE)
    score_scale = HEAD_SIZE ** (-0.5)
    cached = (
        jnp.einsum(
            "rkgd,rlkd->rkgl", heads_of_queries, heads_of_keys, preferred_element_type=jnp.float32
        )
        * score_scale
    )
    fresh = (
        jnp.einsum(
            "rkgd,rkd->rkg", heads_of_queries, newest_key, preferred_element_type=jnp.float32
        )
        * score_scale
    )
    valid_mask = jnp.arange(span_length, dtype=jnp.int32)[None, :] < context_length_per_row[:, None]
    cached = jnp.where(valid_mask[:, None, None, :], cached, jnp.float32(-1e30))
    top_score = jnp.maximum(jnp.max(cached, axis=-1), fresh)
    exp_cached = jnp.exp(cached - top_score[..., None])
    exp_fresh = jnp.exp(fresh - top_score)
    denominator = jnp.sum(exp_cached, axis=-1) + exp_fresh
    prob_cached = (exp_cached / denominator[..., None]).astype(jnp.bfloat16)
    prob_fresh = (exp_fresh / denominator).astype(jnp.bfloat16)
    mixed = jnp.einsum(
        "rkgl,rlkd->rkgd", prob_cached, heads_of_values, preferred_element_type=jnp.float32
    )
    mixed = (
        mixed
        + prob_fresh.astype(jnp.float32)[..., None]
        * newest_value.astype(jnp.float32)[:, :, None, :]
    )
    return mixed.reshape(count_of_rows, QUERY_HEADS * HEAD_SIZE)


def weight_columns(chosen_ids, gate_weights, expert_count):
    experts = jnp.arange(expert_count, dtype=jnp.int32)
    table = jnp.sum(
        jnp.where(chosen_ids[:, :, None] == experts, gate_weights[:, :, None], 0.0), axis=1
    )
    high = table.astype(jnp.bfloat16)
    low = (table - high.astype(jnp.float32)).astype(jnp.bfloat16)
    columns = jnp.concatenate([high, low], axis=1)
    return jnp.pad(columns, ((0, 0), (0, -columns.shape[1] % 128)))


def on_device(
    queries,
    cached_key_table,
    cached_value_table,
    incoming_keys,
    incoming_values,
    context_length_per_row,
    residual,
    norm_gain,
    expert_ids,
    gate_weights,
    gate_proj,
    up_proj,
    down_proj,
):
    count_of_rows, width = residual.shape
    expert_count = lax.axis_size("dev")
    attn = attend(
        queries,
        cached_key_table,
        cached_value_table,
        incoming_keys,
        incoming_values,
        context_length_per_row,
    )
    hidden = (residual.astype(jnp.float32) + attn).astype(jnp.bfloat16)
    wide = hidden.astype(jnp.float32)
    mean_square = jnp.mean(wide * wide, axis=-1, keepdims=True)
    normed = (wide * lax.rsqrt(mean_square + 1e-06) * norm_gain.astype(jnp.float32)).astype(
        jnp.bfloat16
    )
    mine = lax.axis_index("dev")
    sent = jnp.concatenate([normed, weight_columns(expert_ids, gate_weights, expert_count)], axis=1)
    rows = gather_rows(sent)
    tail = rows[:, width:].astype(jnp.float32)
    places = jnp.arange(tail.shape[1], dtype=jnp.int32)
    weight = jnp.sum(
        jnp.where((places == mine) | (places == mine + expert_count), tail, 0.0),
        axis=1,
        keepdims=True,
    )
    rows = rows[:, :width]
    gate_val = jnp.dot(rows, gate_proj[0], preferred_element_type=jnp.float32)
    up_val = jnp.dot(rows, up_proj[0], preferred_element_type=jnp.float32)
    act = (jax.nn.silu(gate_val) * up_val).astype(jnp.bfloat16)
    part = jnp.dot(act, down_proj[0], preferred_element_type=jnp.float32)
    part = (part * weight).astype(jnp.bfloat16)
    summed = sum_rows(part.reshape(-1, count_of_rows, width))
    return (hidden.astype(jnp.float32) + summed).astype(jnp.bfloat16)


def solution(mesh):
    in_specs = (
        P(("side", "dev"), None),
        P(("side", "dev"), None, None),
        P(("side", "dev"), None, None),
        P(("side", "dev"), None),
        P(("side", "dev"), None),
        P(("side", "dev")),
        P(("side", "dev"), None),
        P(),
        P(("side", "dev"), None),
        P(("side", "dev"), None),
        P("dev", None, "side"),
        P("dev", None, "side"),
        P("dev", "side", None),
    )
    out_specs = P(("side", "dev"), None)
    return jax.shard_map(
        on_device, mesh=mesh, in_specs=in_specs, out_specs=out_specs, check_vma=False
    )
```

```python
import functools

import jax
import jax.numpy as jnp
from jax import lax
from jax.experimental import pallas as pl
from jax.experimental.pallas import tpu as pltpu
from jax.sharding import PartitionSpec as P

QUERY_HEADS = 32
KEY_VALUE_HEADS = 2
HEAD_SIZE = 128
MESH = pl.DeviceIdType.MESH
VMEM_LIMIT = 60 * 1024 * 1024


def grid_of(count):
    return {16: (4, 2, 2), 64: (4, 4, 4)}.get(count, (count, 1, 1))


def halves_of(width):
    first = width // 256 * 128
    return (slice(0, first), slice(first, width))


class Links:
    def __init__(self, sizes):
        self.sizes = sizes
        me = lax.axis_index("dev")
        self.side = lax.axis_index("side")
        self.at = (me // (sizes[1] * sizes[2]), me // sizes[2] % sizes[1], me % sizes[2])
        self.started = []

    def moved(self, steps):
        spot = [(a + n + d) % n for a, d, n in zip(self.at, steps, self.sizes)]
        return (spot[0] * self.sizes[1] + spot[1]) * self.sizes[2] + spot[2]

    def along(self, axis, step):
        return {"dev": self.moved(tuple(step if i == axis else 0 for i in range(3)))}

    def other(self):
        return {"side": 1 - self.side}

    def barrier(self):
        semaphore = pltpu.get_barrier_semaphore()
        peers = [self.other()]
        for axis in range(3):
            peers += [self.along(axis, step) for step in range(1, self.sizes[axis])]
        for peer in peers:
            pl.semaphore_signal(semaphore, inc=1, device_id=peer, device_id_type=MESH)
        pl.semaphore_wait(semaphore, len(peers))

    def copy(self, source, target, send_sems, recv_sem, peer):
        sent = pltpu.make_async_remote_copy(
            src_ref=source,
            dst_ref=target,
            send_sem=send_sems.at[len(self.started)],
            recv_sem=recv_sem,
            device_id=peer,
            device_id_type=MESH,
        )
        sent.start()
        self.started.append(sent)

    def arrived(self, target, send_sems, recv_sem):
        pltpu.make_async_remote_copy(
            src_ref=target,
            dst_ref=target,
            send_sem=send_sems.at[0],
            recv_sem=recv_sem,
            device_id=self.other(),
            device_id_type=MESH,
        ).wait_recv()

    def finish(self):
        for sent in self.started:
            sent.wait_send()


def gather_kernel(sizes, own_ref, all_ref, send_sems, near_sems, mid_sems, far_sems, side_sems):
    n0, n1, n2 = sizes
    count = n0 * n1 * n2
    links = Links(sizes)
    cuts = halves_of(own_ref.shape[1])
    links.barrier()

    def block(steps, half, side=None):
        base = (links.side if side is None else side) * count
        return all_ref.at[base + links.moved(steps), :, cuts[half]]

    def source(steps, half):
        return own_ref.at[:, cuts[half]] if steps == (0, 0, 0) else block(steps, half)

    def relative(steps):
        back = [-d % n for d, n in zip(steps, sizes)]
        return (back[0] * n1 + back[1]) * n2 + back[2]

    def cross(steps, half):
        links.copy(
            source(steps, half), block(steps, half), send_sems,
            side_sems.at[half, relative(steps)], links.other(),
        )

    def spread(steps, half, axis, sems, slot):
        for k in range(1, sizes[axis]):
            links.copy(
                source(steps, half), block(steps, half), send_sems,
                sems.at[half, slot * max(sizes) + k], links.along(axis, k),
            )

    first, second = (2, 1), (1, 2)
    for half in range(2):
        for k in range(1, n0):
            links.copy(
                source((0, 0, 0), half), block((0, 0, 0), half), send_sems,
                near_sems.at[half, k], links.along(0, k),
            )
    for j in range(n0):
        for half in range(2):
            steps = (-j, 0, 0)
            if j:
                links.arrived(block(steps, half), send_sems, near_sems.at[half, j])
            spread(steps, half, first[half], mid_sems, j)
            spread(steps, half, second[half], far_sems, j * max(sizes))
            cross(steps, half)

    def shifted(j, half, mid, far):
        steps = [-j, 0, 0]
        steps[first[half]] = -mid
        steps[second[half]] = -far
        return tuple(steps)

    for j in range(n0):
        for half in range(2):
            for k in range(1, sizes[first[half]]):
                steps = shifted(j, half, k, 0)
                links.arrived(block(steps, half), send_sems, mid_sems.at[half, j * max(sizes) + k])
                spread(steps, half, second[half], far_sems, j * max(sizes) + k)
                cross(steps, half)
    for j in range(n0):
        for c in range(max(sizes)):
            for half in range(2):
                if c >= sizes[first[half]]:
                    continue
                for k in range(1, sizes[second[half]]):
                    steps = shifted(j, half, c, k)
                    slot = (j * max(sizes) + c) * max(sizes) + k
                    links.arrived(block(steps, half), send_sems, far_sems.at[half, slot])
                    cross(steps, half)
    all_ref[links.side * count + links.moved((0, 0, 0))] = own_ref[...]
    for j in range(n0):
        for b in range(n1):
            for c in range(n2):
                for half in range(2):
                    steps = (-j, -b, -c)
                    links.arrived(
                        block(steps, half, 1 - links.side), send_sems,
                        side_sems.at[half, relative(steps)],
                    )
    links.finish()


def gather_rows(own):
    count = lax.axis_size("dev")
    sizes = grid_of(count)
    wide = max(sizes)
    rows, width = own.shape
    dma = pltpu.SemaphoreType.DMA
    sends = 2 * (count - 1) + 2 * count
    return pl.pallas_call(
        functools.partial(gather_kernel, sizes),
        out_shape=jax.ShapeDtypeStruct((2 * count, rows, width), own.dtype),
        in_specs=[pl.BlockSpec(memory_space=pltpu.VMEM)],
        out_specs=pl.BlockSpec(memory_space=pltpu.VMEM),
        scratch_shapes=[
            dma((sends,)),
            dma((2, wide)),
            dma((2, wide * wide)),
            dma((2, wide * wide * wide)),
            dma((2, count)),
        ],
        compiler_params=pltpu.CompilerParams(
            collective_id=0, has_side_effects=True, vmem_limit_bytes=VMEM_LIMIT
        ),
        name="gather_rows",
    )(own).reshape(2 * count * rows, width)


def sum_kernel(
    sizes, part_ref, out_ref, acc, from_side, from_far, from_mid, from_near,
    send_sems, side_sems, far_sems, mid_sems, near_sems,
):
    n0, n1, n2 = sizes
    count = n0 * n1 * n2
    wide = max(sizes)
    links = Links(sizes)
    cuts = halves_of(out_ref.shape[1])
    first, second = (2, 1), (1, 2)
    links.barrier()
    order = [(j, b, c) for b in range(n1 - 1, -1, -1) for c in range(n2 - 1, -1, -1) for j in range(n0)]

    def mine(steps):
        return links.moved(steps)

    for i, steps in enumerate(order):
        links.copy(
            part_ref.at[(1 - links.side) * count + mine(steps)], from_side.at[i],
            send_sems, side_sems.at[i], links.other(),
        )

    def total(left, right):
        return (left.astype(jnp.float32) + right.astype(jnp.float32)).astype(jnp.bfloat16)

    for i, steps in enumerate(order):
        spot = mine(steps)
        links.arrived(from_side.at[i], send_sems, side_sems.at[i])
        acc[spot] = total(part_ref[links.side * count + spot], from_side[i])
        for half in range(2):
            k = steps[second[half]]
            if k:
                slot = (steps[0] * wide + steps[first[half]]) * wide + k
                links.copy(
                    acc.at[spot, :, cuts[half]], from_far.at[half, slot],
                    send_sems, far_sems.at[half, slot], links.along(second[half], k),
                )

    def shifted(j, half, mid):
        steps = [j, 0, 0]
        steps[first[half]] = mid
        return tuple(steps)

    for c in range(wide - 1, -1, -1):
        for j in range(n0):
            for half in range(2):
                if c >= sizes[first[half]]:
                    continue
                spot = mine(shifted(j, half, c))
                for k in range(1, sizes[second[half]]):
                    slot = (j * wide + c) * wide + k
                    links.arrived(from_far.at[half, slot], send_sems, far_sems.at[half, slot])
                    acc[spot, :, cuts[half]] = total(
                        acc[spot, :, cuts[half]], from_far[half, slot]
                    )
                if c:
                    slot = j * wide + c
                    links.copy(
                        acc.at[spot, :, cuts[half]], from_mid.at[half, slot],
                        send_sems, mid_sems.at[half, slot], links.along(first[half], c),
                    )
    for j in range(n0 - 1, -1, -1):
        for half in range(2):
            spot = mine((j, 0, 0))
            for k in range(1, sizes[first[half]]):
                slot = j * wide + k
                links.arrived(from_mid.at[half, slot], send_sems, mid_sems.at[half, slot])
                acc[spot, :, cuts[half]] = total(acc[spot, :, cuts[half]], from_mid[half, slot])
            if j:
                links.copy(
                    acc.at[spot, :, cuts[half]], from_near.at[half, j],
                    send_sems, near_sems.at[half, j], links.along(0, j),
                )
    for half in range(2):
        value = acc[mine((0, 0, 0)), :, cuts[half]].astype(jnp.float32)
        for k in range(1, n0):
            links.arrived(from_near.at[half, k], send_sems, near_sems.at[half, k])
            value = value + from_near[half, k].astype(jnp.float32)
        out_ref[:, cuts[half]] = value
    links.finish()


def sum_rows(part):
    count = lax.axis_size("dev")
    sizes = grid_of(count)
    wide = max(sizes)
    _, rows, width = part.shape
    dma = pltpu.SemaphoreType.DMA
    slots = sizes[0] * wide
    return pl.pallas_call(
        functools.partial(sum_kernel, sizes),
        out_shape=jax.ShapeDtypeStruct((rows, width), jnp.float32),
        in_specs=[pl.BlockSpec(memory_space=pltpu.VMEM)],
        out_specs=pl.BlockSpec(memory_space=pltpu.VMEM),
        scratch_shapes=[
            pltpu.VMEM((count, rows, width), part.dtype),
            pltpu.VMEM((count, rows, width), part.dtype),
            pltpu.VMEM((2, slots * wide, rows, width // 2), part.dtype),
            pltpu.VMEM((2, slots, rows, width // 2), part.dtype),
            pltpu.VMEM((2, sizes[0], rows, width // 2), part.dtype),
            dma((count + 2 * (count - 1),)),
            dma((count,)),
            dma((2, slots * wide)),
            dma((2, slots)),
            dma((2, sizes[0])),
        ],
        compiler_params=pltpu.CompilerParams(
            collective_id=1, has_side_effects=True, vmem_limit_bytes=VMEM_LIMIT
        ),
        name="sum_rows",
    )(part)


def gather_steps(sizes, links, halfway, own_ref, all_ref, send_sems, near_sems, mid_sems, far_sems, side_sems):
    n0, n1, n2 = sizes
    count = n0 * n1 * n2
    cuts = halves_of(own_ref.shape[1])

    def block(steps, half, side=None):
        base = (links.side if side is None else side) * count
        return all_ref.at[base + links.moved(steps), :, cuts[half]]

    def source(steps, half):
        return own_ref.at[:, cuts[half]] if steps == (0, 0, 0) else block(steps, half)

    def relative(steps):
        back = [-d % n for d, n in zip(steps, sizes)]
        return (back[0] * n1 + back[1]) * n2 + back[2]

    def cross(steps, half):
        links.copy(
            source(steps, half), block(steps, half), send_sems,
            side_sems.at[half, relative(steps)], links.other(),
        )

    def spread(steps, half, axis, sems, slot):
        for k in range(1, sizes[axis]):
            links.copy(
                source(steps, half), block(steps, half), send_sems,
                sems.at[half, slot * max(sizes) + k], links.along(axis, k),
            )

    first, second = (2, 1), (1, 2)
    for half in range(2):
        for k in range(1, n0):
            links.copy(
                source((0, 0, 0), half), block((0, 0, 0), half), send_sems,
                near_sems.at[half, k], links.along(0, k),
            )
    for j in range(n0):
        for half in range(2):
            steps = (-j, 0, 0)
            if j:
                links.arrived(block(steps, half), send_sems, near_sems.at[half, j])
            spread(steps, half, first[half], mid_sems, j)
            spread(steps, half, second[half], far_sems, j * max(sizes))
            cross(steps, half)

    def shifted(j, half, mid, far):
        steps = [-j, 0, 0]
        steps[first[half]] = -mid
        steps[second[half]] = -far
        return tuple(steps)

    for j in range(n0):
        for half in range(2):
            for k in range(1, sizes[first[half]]):
                steps = shifted(j, half, k, 0)
                links.arrived(block(steps, half), send_sems, mid_sems.at[half, j * max(sizes) + k])
                spread(steps, half, second[half], far_sems, j * max(sizes) + k)
                cross(steps, half)
    all_ref[links.side * count + links.moved((0, 0, 0))] = own_ref[...]
    pending = {(b, c, half) for b in range(n1) for c in range(n2) for half in range(2)}

    def crossed(b, c, half):
        if (b, c, half) in pending:
            pending.remove((b, c, half))
            for j in range(n0):
                steps = (-j, -b, -c)
                links.arrived(
                    block(steps, half, 1 - links.side), send_sems,
                    side_sems.at[half, relative(steps)],
                )

    for c in range(n2):
        crossed(0, c, 0)
    halfway(0)
    for j in range(n0):
        if j == n0 // 2:
            for b in range(n1):
                crossed(b, 0, 1)
            halfway(1)
        for c in range(max(sizes)):
            for half in range(2):
                if c >= sizes[first[half]]:
                    continue
                for k in range(1, sizes[second[half]]):
                    steps = shifted(j, half, c, k)
                    slot = (j * max(sizes) + c) * max(sizes) + k
                    links.arrived(block(steps, half), send_sems, far_sems.at[half, slot])
                    cross(steps, half)
    for b in range(n1):
        for c in range(n2):
            for half in range(2):
                crossed(b, c, half)


def sum_steps(
    sizes, links, ready, part_ref, out_ref, acc, from_side, from_far, from_mid, from_near,
    send_sems, side_sems, far_sems, mid_sems, near_sems,
):
    n0, n1, n2 = sizes
    count = n0 * n1 * n2
    wide = max(sizes)
    cuts = halves_of(out_ref.shape[1])
    first, second = (2, 1), (1, 2)
    order = [(j, b, c) for b in range(n1 - 1, -1, -1) for c in range(n2 - 1, -1, -1) for j in range(n0)]

    def mine(steps):
        return links.moved(steps)

    sent_to = None
    for i, steps in enumerate(order):
        if steps[1] != sent_to:
            sent_to = steps[1]
            ready(sent_to)
        links.copy(
            part_ref.at[(1 - links.side) * count + mine(steps)], from_side.at[i],
            send_sems, side_sems.at[i], links.other(),
        )

    def total(left, right):
        return (left.astype(jnp.float32) + right.astype(jnp.float32)).astype(jnp.bfloat16)

    for i, steps in enumerate(order):
        spot = mine(steps)
        links.arrived(from_side.at[i], send_sems, side_sems.at[i])
        acc[spot] = total(part_ref[links.side * count + spot], from_side[i])
        for half in range(2):
            k = steps[second[half]]
            if k:
                slot = (steps[0] * wide + steps[first[half]]) * wide + k
                links.copy(
                    acc.at[spot, :, cuts[half]], from_far.at[half, slot],
                    send_sems, far_sems.at[half, slot], links.along(second[half], k),
                )

    def shifted(j, half, mid):
        steps = [j, 0, 0]
        steps[first[half]] = mid
        return tuple(steps)

    for c in range(wide - 1, -1, -1):
        for j in range(n0):
            for half in range(2):
                if c >= sizes[first[half]]:
                    continue
                spot = mine(shifted(j, half, c))
                for k in range(1, sizes[second[half]]):
                    slot = (j * wide + c) * wide + k
                    links.arrived(from_far.at[half, slot], send_sems, far_sems.at[half, slot])
                    acc[spot, :, cuts[half]] = total(
                        acc[spot, :, cuts[half]], from_far[half, slot]
                    )
                if c:
                    slot = j * wide + c
                    links.copy(
                        acc.at[spot, :, cuts[half]], from_mid.at[half, slot],
                        send_sems, mid_sems.at[half, slot], links.along(first[half], c),
                    )
    for j in range(n0 - 1, -1, -1):
        for half in range(2):
            spot = mine((j, 0, 0))
            for k in range(1, sizes[first[half]]):
                slot = j * wide + k
                links.arrived(from_mid.at[half, slot], send_sems, mid_sems.at[half, slot])
                acc[spot, :, cuts[half]] = total(acc[spot, :, cuts[half]], from_mid[half, slot])
            if j:
                links.copy(
                    acc.at[spot, :, cuts[half]], from_near.at[half, j],
                    send_sems, near_sems.at[half, j], links.along(0, j),
                )
    for half in range(2):
        value = acc[mine((0, 0, 0)), :, cuts[half]].astype(jnp.float32)
        for k in range(1, n0):
            links.arrived(from_near.at[half, k], send_sems, near_sems.at[half, k])
            value = value + from_near[half, k].astype(jnp.float32)
        out_ref[:, cuts[half]] = value


def layer_kernel(
    sizes, own_ref, gate_hbm, up_hbm, down_hbm, out_ref,
    all_ref, gate_ref, up_ref, down_ref, taken, value, act, part,
    acc, from_side, from_far, from_mid, from_near, weight_sems,
    near_sems, mid_sems, far_sems, side_sems, send_sems,
    back_side_sems, back_far_sems, back_mid_sems, back_near_sems,
):
    n0, n1, n2 = sizes
    count = n0 * n1 * n2
    rows, width = out_ref.shape
    inner = gate_ref.shape[1]
    depth = width // 2
    group = 2 * n0 * rows
    loads = [
        pltpu.make_async_copy(source.at[0], target, weight_sems.at[i])
        for i, (source, target) in enumerate(
            ((gate_hbm, gate_ref), (up_hbm, up_ref), (down_hbm, down_ref))
        )
    ]
    for load in loads:
        load.start()
    links = Links(sizes)
    links.barrier()

    def spots(b, c):
        for s in range(2):
            base = (links.side if s == 0 else 1 - links.side) * count
            for j in range(n0):
                yield (s * n0 + j) * rows, base + links.moved((-j, -b, -c))

    def multiply(half, fixed, first):
        pairs = [(fixed, i) if half == 0 else (i, fixed) for i in range(2)]
        for i, (b, c) in enumerate(pairs):
            for offset, spot in spots(b, c):
                taken[pl.ds(i * group + offset, rows), :] = all_ref[
                    spot, :, pl.ds(half * depth, depth)
                ]

        def column(n, carry):
            at = pl.ds(pl.multiple_of(n * 256, 256), 256)
            for which, matrix in enumerate((gate_ref, up_ref)):
                found = jnp.dot(
                    taken[...], matrix[pl.ds(half * depth, depth), at],
                    preferred_element_type=jnp.float32,
                )
                for i, (b, c) in enumerate(pairs):
                    piece = found[i * group : (i + 1) * group]
                    if not first(b, c):
                        piece = piece + value[which, b, c, :, at]
                    value[which, b, c, :, at] = piece
            return carry

        lax.fori_loop(0, inner // 256, column, 0)

    def halfway(half):
        if half == 0:
            loads[0].wait()
            loads[1].wait()
            multiply(0, 0, lambda b, c: True)
        else:
            multiply(1, 0, lambda b, c: b != 0)

    gather_steps(
        sizes, links, halfway, own_ref, all_ref, send_sems, near_sems, mid_sems, far_sems, side_sems
    )
    multiply(0, 1, lambda b, c: c != 0)
    multiply(1, 1, lambda b, c: False)
    loads[2].wait()

    def ready(b):
        mine = lax.axis_index("dev")
        for c in range(n2):
            for offset, spot in spots(b, c):
                tail = all_ref[spot, :, pl.ds(width, own_ref.shape[1] - width)].astype(jnp.float32)
                places = lax.broadcasted_iota(jnp.int32, tail.shape, 1)
                chosen = (places == mine) | (places == mine + count)
                weight = jnp.sum(jnp.where(chosen, tail, 0.0), axis=1, keepdims=True)
                gate_val = value[0, b, c, pl.ds(offset, rows), :]
                up_val = value[1, b, c, pl.ds(offset, rows), :]
                mixed = gate_val / (1.0 + jnp.exp(-gate_val)) * up_val
                act[pl.ds(c * group + offset, rows), :] = (mixed * weight).astype(act.dtype)

        def column(n, carry):
            at = pl.ds(pl.multiple_of(n * 512, 512), 512)
            found = jnp.dot(act[...], down_ref[:, at], preferred_element_type=jnp.float32)
            found = found.astype(part.dtype)
            for c in range(n2):
                for offset, spot in spots(b, c):
                    start = c * group + offset
                    part[spot, :, at] = found[start : start + rows]
            return carry

        lax.fori_loop(0, width // 512, column, 0)

    sum_steps(
        sizes, links, ready, part, out_ref, acc, from_side, from_far, from_mid, from_near,
        send_sems, back_side_sems, back_far_sems, back_mid_sems, back_near_sems,
    )
    links.finish()


def fused_layer(own, gate_proj, up_proj, down_proj):
    count = lax.axis_size("dev")
    sizes = grid_of(count)
    wide = max(sizes)
    rows = own.shape[0]
    _, width, inner = gate_proj.shape
    slots = sizes[0] * wide
    group = 2 * sizes[0] * rows
    kind = own.dtype
    dma = pltpu.SemaphoreType.DMA
    return pl.pallas_call(
        functools.partial(layer_kernel, sizes),
        out_shape=jax.ShapeDtypeStruct((rows, width), jnp.float32),
        in_specs=[pl.BlockSpec(memory_space=pltpu.VMEM)]
        + [pl.BlockSpec(memory_space=pl.ANY)] * 3,
        out_specs=pl.BlockSpec(memory_space=pltpu.VMEM),
        scratch_shapes=[
            pltpu.VMEM((2 * count,) + own.shape, kind),
            pltpu.VMEM((width, inner), kind),
            pltpu.VMEM((width, inner), kind),
            pltpu.VMEM((inner, width), kind),
            pltpu.VMEM((2 * group, width // 2), kind),
            pltpu.VMEM((2, 2, 2, group, inner), jnp.float32),
            pltpu.VMEM((2 * group, inner), kind),
            pltpu.VMEM((2 * count, rows, width), kind),
            pltpu.VMEM((count, rows, width), kind),
            pltpu.VMEM((count, rows, width), kind),
            pltpu.VMEM((2, slots * wide, rows, width // 2), kind),
            pltpu.VMEM((2, slots, rows, width // 2), kind),
            pltpu.VMEM((2, sizes[0], rows, width // 2), kind),
            dma((3,)),
            dma((2, wide)),
            dma((2, slots)),
            dma((2, slots * wide)),
            dma((2, count)),
            dma((4 * (count - 1) + 3 * count,)),
            dma((count,)),
            dma((2, slots * wide)),
            dma((2, slots)),
            dma((2, sizes[0])),
        ],
        compiler_params=pltpu.CompilerParams(
            collective_id=2, has_side_effects=True, vmem_limit_bytes=VMEM_LIMIT
        ),
        name="fused_layer",
    )(own, gate_proj, up_proj, down_proj)


def attend(
    queries,
    cached_key_table,
    cached_value_table,
    incoming_keys,
    incoming_values,
    context_length_per_row,
):
    count_of_rows, span_length, _ = cached_key_table.shape
    heads_of_queries = queries.reshape(
        count_of_rows, KEY_VALUE_HEADS, QUERY_HEADS // KEY_VALUE_HEADS, HEAD_SIZE
    )
    heads_of_keys = cached_key_table.reshape(count_of_rows, span_length, KEY_VALUE_HEADS, HEAD_SIZE)
    heads_of_values = cached_value_table.reshape(
        count_of_rows, span_length, KEY_VALUE_HEADS, HEAD_SIZE
    )
    newest_key = incoming_keys.reshape(count_of_rows, KEY_VALUE_HEADS, HEAD_SIZE)
    newest_value = incoming_values.reshape(count_of_rows, KEY_VALUE_HEADS, HEAD_SIZE)
    score_scale = HEAD_SIZE ** (-0.5)
    cached = (
        jnp.einsum(
            "rkgd,rlkd->rkgl", heads_of_queries, heads_of_keys, preferred_element_type=jnp.float32
        )
        * score_scale
    )
    fresh = (
        jnp.einsum(
            "rkgd,rkd->rkg", heads_of_queries, newest_key, preferred_element_type=jnp.float32
        )
        * score_scale
    )
    valid_mask = jnp.arange(span_length, dtype=jnp.int32)[None, :] < context_length_per_row[:, None]
    cached = jnp.where(valid_mask[:, None, None, :], cached, jnp.float32(-1e30))
    top_score = jnp.maximum(jnp.max(cached, axis=-1), fresh)
    exp_cached = jnp.exp(cached - top_score[..., None])
    exp_fresh = jnp.exp(fresh - top_score)
    denominator = jnp.sum(exp_cached, axis=-1) + exp_fresh
    prob_cached = (exp_cached / denominator[..., None]).astype(jnp.bfloat16)
    prob_fresh = (exp_fresh / denominator).astype(jnp.bfloat16)
    mixed = jnp.einsum(
        "rkgl,rlkd->rkgd", prob_cached, heads_of_values, preferred_element_type=jnp.float32
    )
    mixed = (
        mixed
        + prob_fresh.astype(jnp.float32)[..., None]
        * newest_value.astype(jnp.float32)[:, :, None, :]
    )
    return mixed.reshape(count_of_rows, QUERY_HEADS * HEAD_SIZE)


def weight_columns(chosen_ids, gate_weights, expert_count):
    experts = jnp.arange(expert_count, dtype=jnp.int32)
    table = jnp.sum(
        jnp.where(chosen_ids[:, :, None] == experts, gate_weights[:, :, None], 0.0), axis=1
    )
    high = table.astype(jnp.bfloat16)
    low = (table - high.astype(jnp.float32)).astype(jnp.bfloat16)
    columns = jnp.concatenate([high, low], axis=1)
    return jnp.pad(columns, ((0, 0), (0, -columns.shape[1] % 128)))


def on_device(
    queries,
    cached_key_table,
    cached_value_table,
    incoming_keys,
    incoming_values,
    context_length_per_row,
    residual,
    norm_gain,
    expert_ids,
    gate_weights,
    gate_proj,
    up_proj,
    down_proj,
):
    count_of_rows, width = residual.shape
    expert_count = lax.axis_size("dev")
    attn = attend(
        queries,
        cached_key_table,
        cached_value_table,
        incoming_keys,
        incoming_values,
        context_length_per_row,
    )
    hidden = (residual.astype(jnp.float32) + attn).astype(jnp.bfloat16)
    wide = hidden.astype(jnp.float32)
    mean_square = jnp.mean(wide * wide, axis=-1, keepdims=True)
    normed = (wide * lax.rsqrt(mean_square + 1e-06) * norm_gain.astype(jnp.float32)).astype(
        jnp.bfloat16
    )
    mine = lax.axis_index("dev")
    sent = jnp.concatenate([normed, weight_columns(expert_ids, gate_weights, expert_count)], axis=1)
    if grid_of(expert_count)[1:] == (2, 2):
        summed = fused_layer(sent, gate_proj, up_proj, down_proj)
        return (hidden.astype(jnp.float32) + summed).astype(jnp.bfloat16)
    rows = gather_rows(sent)
    tail = rows[:, width:].astype(jnp.float32)
    places = jnp.arange(tail.shape[1], dtype=jnp.int32)
    weight = jnp.sum(
        jnp.where((places == mine) | (places == mine + expert_count), tail, 0.0),
        axis=1,
        keepdims=True,
    )
    rows = rows[:, :width]
    gate_val = jnp.dot(rows, gate_proj[0], preferred_element_type=jnp.float32)
    up_val = jnp.dot(rows, up_proj[0], preferred_element_type=jnp.float32)
    act = (jax.nn.silu(gate_val) * up_val).astype(jnp.bfloat16)
    part = jnp.dot(act, down_proj[0], preferred_element_type=jnp.float32)
    part = (part * weight).astype(jnp.bfloat16)
    summed = sum_rows(part.reshape(-1, count_of_rows, width))
    return (hidden.astype(jnp.float32) + summed).astype(jnp.bfloat16)


def solution(mesh):
    in_specs = (
        P(("side", "dev"), None),
        P(("side", "dev"), None, None),
        P(("side", "dev"), None, None),
        P(("side", "dev"), None),
        P(("side", "dev"), None),
        P(("side", "dev")),
        P(("side", "dev"), None),
        P(),
        P(("side", "dev"), None),
        P(("side", "dev"), None),
        P("dev", None, "side"),
        P("dev", None, "side"),
        P("dev", "side", None),
    )
    out_specs = P(("side", "dev"), None)
    return jax.shard_map(
        on_device, mesh=mesh, in_specs=in_specs, out_specs=out_specs, check_vma=False
    )
```

```python
import functools

import jax
import jax.numpy as jnp
from jax import lax
from jax.experimental import pallas as pl
from jax.experimental.pallas import tpu as pltpu
from jax.sharding import PartitionSpec as P

QUERY_HEADS = 32
KEY_VALUE_HEADS = 2
HEAD_SIZE = 128
MESH = pl.DeviceIdType.MESH
VMEM_LIMIT = 60 * 1024 * 1024


def grid_of(count):
    return {16: (4, 2, 2), 64: (4, 4, 4)}.get(count, (count, 1, 1))


def halves_of(width):
    first = width // 256 * 128
    return (slice(0, first), slice(first, width))


class Links:
    def __init__(self, sizes):
        self.sizes = sizes
        me = lax.axis_index("dev")
        self.side = lax.axis_index("side")
        self.at = (me // (sizes[1] * sizes[2]), me // sizes[2] % sizes[1], me % sizes[2])
        self.started = []

    def moved(self, steps):
        spot = [(a + n + d) % n for a, d, n in zip(self.at, steps, self.sizes)]
        return (spot[0] * self.sizes[1] + spot[1]) * self.sizes[2] + spot[2]

    def along(self, axis, step):
        return {"dev": self.moved(tuple(step if i == axis else 0 for i in range(3)))}

    def other(self):
        return {"side": 1 - self.side}

    def barrier(self):
        semaphore = pltpu.get_barrier_semaphore()
        peers = [self.other()]
        for axis in range(3):
            peers += [self.along(axis, step) for step in range(1, self.sizes[axis])]
        for peer in peers:
            pl.semaphore_signal(semaphore, inc=1, device_id=peer, device_id_type=MESH)
        pl.semaphore_wait(semaphore, len(peers))

    def copy(self, source, target, send_sems, recv_sem, peer):
        sent = pltpu.make_async_remote_copy(
            src_ref=source,
            dst_ref=target,
            send_sem=send_sems.at[len(self.started)],
            recv_sem=recv_sem,
            device_id=peer,
            device_id_type=MESH,
        )
        sent.start()
        self.started.append(sent)

    def arrived(self, target, send_sems, recv_sem):
        pltpu.make_async_remote_copy(
            src_ref=target,
            dst_ref=target,
            send_sem=send_sems.at[0],
            recv_sem=recv_sem,
            device_id=self.other(),
            device_id_type=MESH,
        ).wait_recv()

    def finish(self):
        for sent in self.started:
            sent.wait_send()


def gather_kernel(sizes, own_ref, all_ref, send_sems, near_sems, mid_sems, far_sems, side_sems):
    n0, n1, n2 = sizes
    count = n0 * n1 * n2
    links = Links(sizes)
    cuts = halves_of(own_ref.shape[1])
    links.barrier()

    def block(steps, half, side=None):
        base = (links.side if side is None else side) * count
        return all_ref.at[base + links.moved(steps), :, cuts[half]]

    def source(steps, half):
        return own_ref.at[:, cuts[half]] if steps == (0, 0, 0) else block(steps, half)

    def relative(steps):
        back = [-d % n for d, n in zip(steps, sizes)]
        return (back[0] * n1 + back[1]) * n2 + back[2]

    def cross(steps, half):
        links.copy(
            source(steps, half), block(steps, half), send_sems,
            side_sems.at[half, relative(steps)], links.other(),
        )

    def spread(steps, half, axis, sems, slot):
        for k in range(1, sizes[axis]):
            links.copy(
                source(steps, half), block(steps, half), send_sems,
                sems.at[half, slot * max(sizes) + k], links.along(axis, k),
            )

    first, second = (2, 1), (1, 2)
    for half in range(2):
        for k in range(1, n0):
            links.copy(
                source((0, 0, 0), half), block((0, 0, 0), half), send_sems,
                near_sems.at[half, k], links.along(0, k),
            )
    for j in range(n0):
        for half in range(2):
            steps = (-j, 0, 0)
            if j:
                links.arrived(block(steps, half), send_sems, near_sems.at[half, j])
            spread(steps, half, first[half], mid_sems, j)
            spread(steps, half, second[half], far_sems, j * max(sizes))
            cross(steps, half)

    def shifted(j, half, mid, far):
        steps = [-j, 0, 0]
        steps[first[half]] = -mid
        steps[second[half]] = -far
        return tuple(steps)

    for j in range(n0):
        for half in range(2):
            for k in range(1, sizes[first[half]]):
                steps = shifted(j, half, k, 0)
                links.arrived(block(steps, half), send_sems, mid_sems.at[half, j * max(sizes) + k])
                spread(steps, half, second[half], far_sems, j * max(sizes) + k)
                cross(steps, half)
    for j in range(n0):
        for c in range(max(sizes)):
            for half in range(2):
                if c >= sizes[first[half]]:
                    continue
                for k in range(1, sizes[second[half]]):
                    steps = shifted(j, half, c, k)
                    slot = (j * max(sizes) + c) * max(sizes) + k
                    links.arrived(block(steps, half), send_sems, far_sems.at[half, slot])
                    cross(steps, half)
    all_ref[links.side * count + links.moved((0, 0, 0))] = own_ref[...]
    for j in range(n0):
        for b in range(n1):
            for c in range(n2):
                for half in range(2):
                    steps = (-j, -b, -c)
                    links.arrived(
                        block(steps, half, 1 - links.side), send_sems,
                        side_sems.at[half, relative(steps)],
                    )
    links.finish()


def gather_rows(own):
    count = lax.axis_size("dev")
    sizes = grid_of(count)
    wide = max(sizes)
    rows, width = own.shape
    dma = pltpu.SemaphoreType.DMA
    sends = 2 * (count - 1) + 2 * count
    return pl.pallas_call(
        functools.partial(gather_kernel, sizes),
        out_shape=jax.ShapeDtypeStruct((2 * count, rows, width), own.dtype),
        in_specs=[pl.BlockSpec(memory_space=pltpu.VMEM)],
        out_specs=pl.BlockSpec(memory_space=pltpu.VMEM),
        scratch_shapes=[
            dma((sends,)),
            dma((2, wide)),
            dma((2, wide * wide)),
            dma((2, wide * wide * wide)),
            dma((2, count)),
        ],
        compiler_params=pltpu.CompilerParams(
            collective_id=0, has_side_effects=True, vmem_limit_bytes=VMEM_LIMIT
        ),
        name="gather_rows",
    )(own).reshape(2 * count * rows, width)


def sum_kernel(
    sizes, part_ref, out_ref, acc, from_side, from_far, from_mid, from_near,
    send_sems, side_sems, far_sems, mid_sems, near_sems,
):
    n0, n1, n2 = sizes
    count = n0 * n1 * n2
    wide = max(sizes)
    links = Links(sizes)
    cuts = halves_of(out_ref.shape[1])
    first, second = (2, 1), (1, 2)
    links.barrier()
    order = [(j, b, c) for b in range(n1 - 1, -1, -1) for c in range(n2 - 1, -1, -1) for j in range(n0)]

    def mine(steps):
        return links.moved(steps)

    for i, steps in enumerate(order):
        links.copy(
            part_ref.at[(1 - links.side) * count + mine(steps)], from_side.at[i],
            send_sems, side_sems.at[i], links.other(),
        )

    def total(left, right):
        return (left.astype(jnp.float32) + right.astype(jnp.float32)).astype(jnp.bfloat16)

    for i, steps in enumerate(order):
        spot = mine(steps)
        links.arrived(from_side.at[i], send_sems, side_sems.at[i])
        acc[spot] = total(part_ref[links.side * count + spot], from_side[i])
        for half in range(2):
            k = steps[second[half]]
            if k:
                slot = (steps[0] * wide + steps[first[half]]) * wide + k
                links.copy(
                    acc.at[spot, :, cuts[half]], from_far.at[half, slot],
                    send_sems, far_sems.at[half, slot], links.along(second[half], k),
                )

    def shifted(j, half, mid):
        steps = [j, 0, 0]
        steps[first[half]] = mid
        return tuple(steps)

    for c in range(wide - 1, -1, -1):
        for j in range(n0):
            for half in range(2):
                if c >= sizes[first[half]]:
                    continue
                spot = mine(shifted(j, half, c))
                for k in range(1, sizes[second[half]]):
                    slot = (j * wide + c) * wide + k
                    links.arrived(from_far.at[half, slot], send_sems, far_sems.at[half, slot])
                    acc[spot, :, cuts[half]] = total(
                        acc[spot, :, cuts[half]], from_far[half, slot]
                    )
                if c:
                    slot = j * wide + c
                    links.copy(
                        acc.at[spot, :, cuts[half]], from_mid.at[half, slot],
                        send_sems, mid_sems.at[half, slot], links.along(first[half], c),
                    )
    for j in range(n0 - 1, -1, -1):
        for half in range(2):
            spot = mine((j, 0, 0))
            for k in range(1, sizes[first[half]]):
                slot = j * wide + k
                links.arrived(from_mid.at[half, slot], send_sems, mid_sems.at[half, slot])
                acc[spot, :, cuts[half]] = total(acc[spot, :, cuts[half]], from_mid[half, slot])
            if j:
                links.copy(
                    acc.at[spot, :, cuts[half]], from_near.at[half, j],
                    send_sems, near_sems.at[half, j], links.along(0, j),
                )
    for half in range(2):
        value = acc[mine((0, 0, 0)), :, cuts[half]].astype(jnp.float32)
        for k in range(1, n0):
            links.arrived(from_near.at[half, k], send_sems, near_sems.at[half, k])
            value = value + from_near[half, k].astype(jnp.float32)
        out_ref[:, cuts[half]] = value
    links.finish()


def sum_rows(part):
    count = lax.axis_size("dev")
    sizes = grid_of(count)
    wide = max(sizes)
    _, rows, width = part.shape
    dma = pltpu.SemaphoreType.DMA
    slots = sizes[0] * wide
    return pl.pallas_call(
        functools.partial(sum_kernel, sizes),
        out_shape=jax.ShapeDtypeStruct((rows, width), jnp.float32),
        in_specs=[pl.BlockSpec(memory_space=pltpu.VMEM)],
        out_specs=pl.BlockSpec(memory_space=pltpu.VMEM),
        scratch_shapes=[
            pltpu.VMEM((count, rows, width), part.dtype),
            pltpu.VMEM((count, rows, width), part.dtype),
            pltpu.VMEM((2, slots * wide, rows, width // 2), part.dtype),
            pltpu.VMEM((2, slots, rows, width // 2), part.dtype),
            pltpu.VMEM((2, sizes[0], rows, width // 2), part.dtype),
            dma((count + 2 * (count - 1),)),
            dma((count,)),
            dma((2, slots * wide)),
            dma((2, slots)),
            dma((2, sizes[0])),
        ],
        compiler_params=pltpu.CompilerParams(
            collective_id=1, has_side_effects=True, vmem_limit_bytes=VMEM_LIMIT
        ),
        name="sum_rows",
    )(part)


def gather_steps(sizes, links, halfway, own_ref, all_ref, send_sems, near_sems, mid_sems, far_sems, side_sems):
    n0, n1, n2 = sizes
    count = n0 * n1 * n2
    cuts = halves_of(own_ref.shape[1])

    def block(steps, half, side=None):
        base = (links.side if side is None else side) * count
        return all_ref.at[base + links.moved(steps), :, cuts[half]]

    def source(steps, half):
        return own_ref.at[:, cuts[half]] if steps == (0, 0, 0) else block(steps, half)

    def relative(steps):
        back = [-d % n for d, n in zip(steps, sizes)]
        return (back[0] * n1 + back[1]) * n2 + back[2]

    def cross(steps, half):
        links.copy(
            source(steps, half), block(steps, half), send_sems,
            side_sems.at[half, relative(steps)], links.other(),
        )

    def spread(steps, half, axis, sems, slot):
        for k in range(1, sizes[axis]):
            links.copy(
                source(steps, half), block(steps, half), send_sems,
                sems.at[half, slot * max(sizes) + k], links.along(axis, k),
            )

    first, second = (2, 1), (1, 2)
    for k in range(1, n0):
        for half in range(2):
            links.copy(
                source((0, 0, 0), half), block((0, 0, 0), half), send_sems,
                near_sems.at[half, k], links.along(0, k),
            )
    def shifted(j, half, mid, far):
        steps = [-j, 0, 0]
        steps[first[half]] = -mid
        steps[second[half]] = -far
        return tuple(steps)

    def from_line(j):
        for half in range(2):
            steps = (-j, 0, 0)
            if j:
                links.arrived(block(steps, half), send_sems, near_sems.at[half, j])
            spread(steps, half, first[half], mid_sems, j)
            spread(steps, half, second[half], far_sems, j * max(sizes))
            cross(steps, half)

    def from_middle(j):
        for half in range(2):
            for k in range(1, sizes[first[half]]):
                steps = shifted(j, half, k, 0)
                links.arrived(block(steps, half), send_sems, mid_sems.at[half, j * max(sizes) + k])
                spread(steps, half, second[half], far_sems, j * max(sizes) + k)
                cross(steps, half)

    from_line(0)
    from_middle(0)
    for j in range(1, n0):
        from_line(j)
        if j > 1:
            from_middle(j - 1)
    from_middle(n0 - 1)
    all_ref[links.side * count + links.moved((0, 0, 0))] = own_ref[...]
    pending = {(b, c, half) for b in range(n1) for c in range(n2) for half in range(2)}

    def crossed(b, c, half):
        if (b, c, half) in pending:
            pending.remove((b, c, half))
            for j in range(n0):
                steps = (-j, -b, -c)
                links.arrived(
                    block(steps, half, 1 - links.side), send_sems,
                    side_sems.at[half, relative(steps)],
                )

    for c in range(n2):
        crossed(0, c, 0)
    halfway(0)
    for j in range(n0):
        if j == n0 // 2:
            for b in range(n1):
                crossed(b, 0, 1)
            halfway(1)
        for c in range(max(sizes)):
            for half in range(2):
                if c >= sizes[first[half]]:
                    continue
                for k in range(1, sizes[second[half]]):
                    steps = shifted(j, half, c, k)
                    slot = (j * max(sizes) + c) * max(sizes) + k
                    links.arrived(block(steps, half), send_sems, far_sems.at[half, slot])
                    cross(steps, half)
    for b in range(n1):
        for c in range(n2):
            for half in range(2):
                crossed(b, c, half)


def sum_steps(
    sizes, links, ready, part_ref, out_ref, acc, from_side, from_far, from_mid, from_near,
    send_sems, side_sems, far_sems, mid_sems, near_sems,
):
    n0, n1, n2 = sizes
    count = n0 * n1 * n2
    wide = max(sizes)
    cuts = halves_of(out_ref.shape[1])
    first, second = (2, 1), (1, 2)
    order = [(j, b, c) for b in range(n1 - 1, -1, -1) for c in range(n2 - 1, -1, -1) for j in range(n0)]

    def mine(steps):
        return links.moved(steps)

    def total(left, right):
        return (left.astype(jnp.float32) + right.astype(jnp.float32)).astype(jnp.bfloat16)

    def cross(b):
        for i, steps in enumerate(order):
            if steps[1] == b:
                links.copy(
                    part_ref.at[(1 - links.side) * count + mine(steps)], from_side.at[i],
                    send_sems, side_sems.at[i], links.other(),
                )

    def fold(b):
        for i, steps in enumerate(order):
            if steps[1] != b:
                continue
            spot = mine(steps)
            links.arrived(from_side.at[i], send_sems, side_sems.at[i])
            acc[spot] = total(part_ref[links.side * count + spot], from_side[i])
            for half in range(2):
                k = steps[second[half]]
                if k:
                    slot = (steps[0] * wide + steps[first[half]]) * wide + k
                    links.copy(
                        acc.at[spot, :, cuts[half]], from_far.at[half, slot],
                        send_sems, far_sems.at[half, slot], links.along(second[half], k),
                    )

    ready(1, 0)
    ready(1, 1)
    cross(1)
    ready(0, 0)
    fold(1)
    ready(0, 1)
    cross(0)
    fold(0)

    def shifted(j, half, mid):
        steps = [j, 0, 0]
        steps[first[half]] = mid
        return tuple(steps)

    for c in range(wide - 1, -1, -1):
        for j in range(n0):
            for half in range(2):
                if c >= sizes[first[half]]:
                    continue
                spot = mine(shifted(j, half, c))
                for k in range(1, sizes[second[half]]):
                    slot = (j * wide + c) * wide + k
                    links.arrived(from_far.at[half, slot], send_sems, far_sems.at[half, slot])
                    acc[spot, :, cuts[half]] = total(
                        acc[spot, :, cuts[half]], from_far[half, slot]
                    )
                if c:
                    slot = j * wide + c
                    links.copy(
                        acc.at[spot, :, cuts[half]], from_mid.at[half, slot],
                        send_sems, mid_sems.at[half, slot], links.along(first[half], c),
                    )
    for j in range(n0 - 1, -1, -1):
        for half in range(2):
            spot = mine((j, 0, 0))
            for k in range(1, sizes[first[half]]):
                slot = j * wide + k
                links.arrived(from_mid.at[half, slot], send_sems, mid_sems.at[half, slot])
                acc[spot, :, cuts[half]] = total(acc[spot, :, cuts[half]], from_mid[half, slot])
            if j:
                links.copy(
                    acc.at[spot, :, cuts[half]], from_near.at[half, j],
                    send_sems, near_sems.at[half, j], links.along(0, j),
                )
    for half in range(2):
        value = acc[mine((0, 0, 0)), :, cuts[half]].astype(jnp.float32)
        for k in range(1, n0):
            links.arrived(from_near.at[half, k], send_sems, near_sems.at[half, k])
            value = value + from_near[half, k].astype(jnp.float32)
        out_ref[:, cuts[half]] = value


def layer_kernel(
    sizes, own_ref, gate_hbm, up_hbm, down_hbm, out_ref,
    all_ref, gate_ref, up_ref, down_ref, taken, value, act, part,
    acc, from_side, from_far, from_mid, from_near, weight_sems,
    near_sems, mid_sems, far_sems, side_sems, send_sems,
    back_side_sems, back_far_sems, back_mid_sems, back_near_sems,
):
    n0, n1, n2 = sizes
    count = n0 * n1 * n2
    rows, width = out_ref.shape
    inner = gate_ref.shape[1]
    depth = width // 2
    group = 2 * n0 * rows
    loads = [
        pltpu.make_async_copy(source.at[0], target, weight_sems.at[i])
        for i, (source, target) in enumerate(
            ((gate_hbm, gate_ref), (up_hbm, up_ref), (down_hbm, down_ref))
        )
    ]
    for load in loads:
        load.start()
    links = Links(sizes)
    links.barrier()

    def spots(b, c):
        for s in range(2):
            base = (links.side if s == 0 else 1 - links.side) * count
            for j in range(n0):
                yield (s * n0 + j) * rows, base + links.moved((-j, -b, -c))

    def multiply(half, fixed, first):
        pairs = [(fixed, i) if half == 0 else (i, fixed) for i in range(2)]
        for i, (b, c) in enumerate(pairs):
            for offset, spot in spots(b, c):
                taken[pl.ds(i * group + offset, rows), :] = all_ref[
                    spot, :, pl.ds(half * depth, depth)
                ]

        def column(n, carry):
            at = pl.ds(pl.multiple_of(n * 256, 256), 256)
            for which, matrix in enumerate((gate_ref, up_ref)):
                found = jnp.dot(
                    taken[...], matrix[pl.ds(half * depth, depth), at],
                    preferred_element_type=jnp.float32,
                )
                for i, (b, c) in enumerate(pairs):
                    piece = found[i * group : (i + 1) * group]
                    if not first(b, c):
                        piece = piece + value[which, b, c, :, at]
                    value[which, b, c, :, at] = piece
            return carry

        lax.fori_loop(0, inner // 256, column, 0)

    def halfway(half):
        if half == 0:
            loads[0].wait()
            loads[1].wait()
            multiply(0, 0, lambda b, c: True)
        else:
            multiply(1, 0, lambda b, c: b != 0)

    gather_steps(
        sizes, links, halfway, own_ref, all_ref, send_sems, near_sems, mid_sems, far_sems, side_sems
    )
    multiply(0, 1, lambda b, c: c != 0)
    multiply(1, 1, lambda b, c: False)
    loads[2].wait()

    def ready(b, turn):
        mine = lax.axis_index("dev")
        for c in range(n2 if turn == 0 else 0):
            for offset, spot in spots(b, c):
                tail = all_ref[spot, :, pl.ds(width, own_ref.shape[1] - width)].astype(jnp.float32)
                places = lax.broadcasted_iota(jnp.int32, tail.shape, 1)
                chosen = (places == mine) | (places == mine + count)
                weight = jnp.sum(jnp.where(chosen, tail, 0.0), axis=1, keepdims=True)
                gate_val = value[0, b, c, pl.ds(offset, rows), :]
                up_val = value[1, b, c, pl.ds(offset, rows), :]
                mixed = gate_val / (1.0 + jnp.exp(-gate_val)) * up_val
                act[pl.ds(c * group + offset, rows), :] = (mixed * weight).astype(act.dtype)

        def column(n, carry):
            at = pl.ds(pl.multiple_of(n * 512, 512), 512)
            found = jnp.dot(act[...], down_ref[:, at], preferred_element_type=jnp.float32)
            found = found.astype(part.dtype)
            for c in range(n2):
                for offset, spot in spots(b, c):
                    start = c * group + offset
                    part[spot, :, at] = found[start : start + rows]
            return carry

        steps = width // 1024
        lax.fori_loop(turn * steps, (turn + 1) * steps, column, 0)

    sum_steps(
        sizes, links, ready, part, out_ref, acc, from_side, from_far, from_mid, from_near,
        send_sems, back_side_sems, back_far_sems, back_mid_sems, back_near_sems,
    )
    links.finish()


def fused_layer(own, gate_proj, up_proj, down_proj):
    count = lax.axis_size("dev")
    sizes = grid_of(count)
    wide = max(sizes)
    rows = own.shape[0]
    _, width, inner = gate_proj.shape
    slots = sizes[0] * wide
    group = 2 * sizes[0] * rows
    kind = own.dtype
    dma = pltpu.SemaphoreType.DMA
    return pl.pallas_call(
        functools.partial(layer_kernel, sizes),
        out_shape=jax.ShapeDtypeStruct((rows, width), jnp.float32),
        in_specs=[pl.BlockSpec(memory_space=pltpu.VMEM)]
        + [pl.BlockSpec(memory_space=pl.ANY)] * 3,
        out_specs=pl.BlockSpec(memory_space=pltpu.VMEM),
        scratch_shapes=[
            pltpu.VMEM((2 * count,) + own.shape, kind),
            pltpu.VMEM((width, inner), kind),
            pltpu.VMEM((width, inner), kind),
            pltpu.VMEM((inner, width), kind),
            pltpu.VMEM((2 * group, width // 2), kind),
            pltpu.VMEM((2, 2, 2, group, inner), jnp.float32),
            pltpu.VMEM((2 * group, inner), kind),
            pltpu.VMEM((2 * count, rows, width), kind),
            pltpu.VMEM((count, rows, width), kind),
            pltpu.VMEM((count, rows, width), kind),
            pltpu.VMEM((2, slots * wide, rows, width // 2), kind),
            pltpu.VMEM((2, slots, rows, width // 2), kind),
            pltpu.VMEM((2, sizes[0], rows, width // 2), kind),
            dma((3,)),
            dma((2, wide)),
            dma((2, slots)),
            dma((2, slots * wide)),
            dma((2, count)),
            dma((4 * (count - 1) + 3 * count,)),
            dma((count,)),
            dma((2, slots * wide)),
            dma((2, slots)),
            dma((2, sizes[0])),
        ],
        compiler_params=pltpu.CompilerParams(
            collective_id=2, has_side_effects=True, vmem_limit_bytes=VMEM_LIMIT
        ),
        name="fused_layer",
    )(own, gate_proj, up_proj, down_proj)


def attend(
    queries,
    cached_key_table,
    cached_value_table,
    incoming_keys,
    incoming_values,
    context_length_per_row,
):
    count_of_rows, span_length, _ = cached_key_table.shape
    heads_of_queries = queries.reshape(
        count_of_rows, KEY_VALUE_HEADS, QUERY_HEADS // KEY_VALUE_HEADS, HEAD_SIZE
    )
    heads_of_keys = cached_key_table.reshape(count_of_rows, span_length, KEY_VALUE_HEADS, HEAD_SIZE)
    heads_of_values = cached_value_table.reshape(
        count_of_rows, span_length, KEY_VALUE_HEADS, HEAD_SIZE
    )
    newest_key = incoming_keys.reshape(count_of_rows, KEY_VALUE_HEADS, HEAD_SIZE)
    newest_value = incoming_values.reshape(count_of_rows, KEY_VALUE_HEADS, HEAD_SIZE)
    score_scale = HEAD_SIZE ** (-0.5)
    cached = (
        jnp.einsum(
            "rkgd,rlkd->rkgl", heads_of_queries, heads_of_keys, preferred_element_type=jnp.float32
        )
        * score_scale
    )
    fresh = (
        jnp.einsum(
            "rkgd,rkd->rkg", heads_of_queries, newest_key, preferred_element_type=jnp.float32
        )
        * score_scale
    )
    valid_mask = jnp.arange(span_length, dtype=jnp.int32)[None, :] < context_length_per_row[:, None]
    cached = jnp.where(valid_mask[:, None, None, :], cached, jnp.float32(-1e30))
    top_score = jnp.maximum(jnp.max(cached, axis=-1), fresh)
    exp_cached = jnp.exp(cached - top_score[..., None])
    exp_fresh = jnp.exp(fresh - top_score)
    denominator = jnp.sum(exp_cached, axis=-1) + exp_fresh
    prob_cached = (exp_cached / denominator[..., None]).astype(jnp.bfloat16)
    prob_fresh = (exp_fresh / denominator).astype(jnp.bfloat16)
    mixed = jnp.einsum(
        "rkgl,rlkd->rkgd", prob_cached, heads_of_values, preferred_element_type=jnp.float32
    )
    mixed = (
        mixed
        + prob_fresh.astype(jnp.float32)[..., None]
        * newest_value.astype(jnp.float32)[:, :, None, :]
    )
    return mixed.reshape(count_of_rows, QUERY_HEADS * HEAD_SIZE)


def weight_columns(chosen_ids, gate_weights, expert_count):
    experts = jnp.arange(expert_count, dtype=jnp.int32)
    table = jnp.sum(
        jnp.where(chosen_ids[:, :, None] == experts, gate_weights[:, :, None], 0.0), axis=1
    )
    high = table.astype(jnp.bfloat16)
    low = (table - high.astype(jnp.float32)).astype(jnp.bfloat16)
    columns = jnp.concatenate([high, low], axis=1)
    return jnp.pad(columns, ((0, 0), (0, -columns.shape[1] % 128)))


def on_device(
    queries,
    cached_key_table,
    cached_value_table,
    incoming_keys,
    incoming_values,
    context_length_per_row,
    residual,
    norm_gain,
    expert_ids,
    gate_weights,
    gate_proj,
    up_proj,
    down_proj,
):
    count_of_rows, width = residual.shape
    expert_count = lax.axis_size("dev")
    attn = attend(
        queries,
        cached_key_table,
        cached_value_table,
        incoming_keys,
        incoming_values,
        context_length_per_row,
    )
    hidden = (residual.astype(jnp.float32) + attn).astype(jnp.bfloat16)
    wide = hidden.astype(jnp.float32)
    mean_square = jnp.mean(wide * wide, axis=-1, keepdims=True)
    normed = (wide * lax.rsqrt(mean_square + 1e-06) * norm_gain.astype(jnp.float32)).astype(
        jnp.bfloat16
    )
    mine = lax.axis_index("dev")
    sent = jnp.concatenate([normed, weight_columns(expert_ids, gate_weights, expert_count)], axis=1)
    if grid_of(expert_count)[1:] == (2, 2):
        summed = fused_layer(sent, gate_proj, up_proj, down_proj)
        return (hidden.astype(jnp.float32) + summed).astype(jnp.bfloat16)
    rows = gather_rows(sent)
    tail = rows[:, width:].astype(jnp.float32)
    places = jnp.arange(tail.shape[1], dtype=jnp.int32)
    weight = jnp.sum(
        jnp.where((places == mine) | (places == mine + expert_count), tail, 0.0),
        axis=1,
        keepdims=True,
    )
    rows = rows[:, :width]
    gate_val = jnp.dot(rows, gate_proj[0], preferred_element_type=jnp.float32)
    up_val = jnp.dot(rows, up_proj[0], preferred_element_type=jnp.float32)
    act = (jax.nn.silu(gate_val) * up_val).astype(jnp.bfloat16)
    part = jnp.dot(act, down_proj[0], preferred_element_type=jnp.float32)
    part = (part * weight).astype(jnp.bfloat16)
    summed = sum_rows(part.reshape(-1, count_of_rows, width))
    return (hidden.astype(jnp.float32) + summed).astype(jnp.bfloat16)


def solution(mesh):
    in_specs = (
        P(("side", "dev"), None),
        P(("side", "dev"), None, None),
        P(("side", "dev"), None, None),
        P(("side", "dev"), None),
        P(("side", "dev"), None),
        P(("side", "dev")),
        P(("side", "dev"), None),
        P(),
        P(("side", "dev"), None),
        P(("side", "dev"), None),
        P("dev", None, "side"),
        P("dev", None, "side"),
        P("dev", "side", None),
    )
    out_specs = P(("side", "dev"), None)
    return jax.shard_map(
        on_device, mesh=mesh, in_specs=in_specs, out_specs=out_specs, check_vma=False
    )
```
